32 devices in a mesh: wave: 4 (over y, core), lev: 8 (over z, x).
Axes of the slice: x: 2, y: 2, z: 4, core: 2. Of those that a mesh axis runs over, the one named last changes fastest.
Arguments:
- spectral: bfloat16 [8, 6, 1280, 1280], P('lev', None, 'wave'), may hold values from -0.16992188 to 0.16992188
- legendre: bfloat16 [1280, 6, 1280], P('wave'), may hold values from -0.15625 to 0.15625
- slot_wave: int32 [1280], replicated, may hold values from 0 to 1279, each once
- cycle_len: int32 [6], replicated, may hold values from 2576 to 5136, as said below
- lat_order: int32 [12], replicated, may hold values from 0 to 11, each once
Outputs:
- grid: float32 [12, 124416], P('wave', 'lev')
The draws below stay inside these ranges and needn't reach their ends.
Inputs may be any that keep to these rules, and one draw needn't show every extreme that they name: `slot_wave`: each wavenumber is held in exactly one slot. `lat_order`: each latitude is held in exactly one row. `cycle_len`: every cycle length is a multiple of 16; some pair has exactly 5136 points and some pair exactly 2576.
All inputs are finite; a program needn't handle non-finite values.
Results may differ from the reference program's by a relative error of at most 0.0003.
Values sent between devices are 32-bit elements; how exact they have to be, the bound alone decides.
A program may use at most 64 MiB of HBM per device.

```python
import math
import jax
import jax.numpy as jnp
from jax import lax

MMAX = 1280
NDEG = 1280
RMAX = 5136
FIELDS = 3
LEVELS = 8
LATW = 12
LATH = 6
RPAD = 5184


def draw_cycle_len(key, part):
    first_key = jax.random.fold_in(key, 11)
    second_key = jax.random.fold_in(key, 12)
    third_key = jax.random.fold_in(key, 13)
    steps_count = (RMAX - (2 * MMAX + 16)) // 16 + 1
    offsets = jax.random.randint(first_key, (LATH,), 0, steps_count)
    lengths = RMAX - 16 * offsets
    longest = jax.random.randint(second_key, (), 0, LATH)
    shortest = (longest + 1 + jax.random.randint(third_key, (), 0, LATH - 1)) % LATH
    positions = jnp.arange(LATH, dtype=jnp.int32)
    lengths = jnp.where(positions == longest, RMAX, lengths)
    lengths = jnp.where(positions == shortest, 2 * MMAX + 16, lengths)
    return lengths.astype(jnp.int32)


def level_of(own_key, shape, pieces, low, top_value):
    level, own = 1.0, jax.random.fold_in(own_key, 6)
    for dim, blocks in pieces:
        draws = jnp.exp(jax.random.uniform(jax.random.fold_in(own, dim), (blocks,), jnp.float32, low / len(pieces), top_value / len(pieces)))
        level = level * jnp.repeat(draws, shape[dim] // blocks).reshape([-1 if axis == dim else 1 for axis in range(len(shape))])
    return level


def centred(stream_key, shape, spread, bound, cuts=(), kind=jnp.bfloat16):
    entries = jax.random.normal(stream_key, shape, jnp.float32) * spread
    if len(cuts) > 0:
        entries = level_of(stream_key, shape, cuts, -0.22, 0.18) * entries
    return jnp.clip(entries, min=-bound, max=bound).astype(kind)


def setup_inputs(seed: int = 0) -> dict:
    streams_of = jax.random.split(jax.random.key(seed), 6)
    spectral = centred(streams_of[0], (LEVELS, 2 * FIELDS, MMAX, NDEG), 0.028, 0.16992188, ((0, 8), (2, 4)))
    legendre = centred(streams_of[1], (MMAX, LATH, NDEG), NDEG ** -0.5, 0.15625, ((0, 4),))
    slot_wave = jax.random.permutation(streams_of[2], MMAX).astype(jnp.int32)
    cycle_len = draw_cycle_len(jax.random.fold_in(streams_of[5], 71), 0)
    lat_order = jax.random.permutation(streams_of[4], LATW).astype(jnp.int32)
    return dict(spectral=spectral, legendre=legendre, slot_wave=slot_wave, cycle_len=cycle_len, lat_order=lat_order)


def cycle_tables(length, count_points):
    waves = jnp.arange(MMAX, dtype=jnp.int32).reshape(MMAX // 16, 16)
    points = jnp.arange(count_points, dtype=jnp.int32)
    phases = (waves[:, :, None] * points[None, None, :]) % length
    angles = (2.0 * math.pi) * phases.astype(jnp.float32) / length.astype(jnp.float32)
    weights = jnp.where(waves == 0, 1.0, 2.0).astype(jnp.float32)[:, :, None]
    return weights * jnp.cos(angles), weights * jnp.sin(angles)


def twiddle():
    residues = jnp.arange(16, dtype=jnp.int32)
    angles = (2.0 * math.pi / 16.0) * ((residues[:, None] * residues[None, :]) % 16).astype(jnp.float32)
    return jnp.cos(angles), jnp.sin(angles)


def place_points(folded, length):
    columns = folded.shape[-1]
    flattened = folded.reshape(folded.shape[:-2] + (16 * columns,))
    points = jnp.arange(RPAD, dtype=jnp.int32)
    period = length // 16
    position = jnp.minimum(points // period, 15) * columns + points % period
    gathered = jnp.take(flattened, position, axis=-1)
    return jnp.where(points < length, gathered, jnp.float32(0.0))


def fold_cycle(coeffs, length):
    highest = lax.Precision.HIGHEST
    cosine, sine = cycle_tables(length, RMAX // 16)
    real_part = coeffs[:, :, 0]
    imag_part = coeffs[:, :, 1]
    inner_real = jnp.einsum("lfab,abp->lfbp", real_part, cosine, precision=highest) - jnp.einsum("lfab,abp->lfbp", imag_part, sine, precision=highest)
    inner_imag = jnp.einsum("lfab,abp->lfbp", real_part, sine, precision=highest) + jnp.einsum("lfab,abp->lfbp", imag_part, cosine, precision=highest)
    twist_cos, twist_sin = twiddle()
    folded = jnp.einsum("lfbp,bq->lfqp", inner_real, twist_cos, precision=highest) - jnp.einsum("lfbp,bq->lfqp", inner_imag, twist_sin, precision=highest)
    return place_points(folded, length)


def legendre_block(inputs):
    spec_block, table_block, wave_block = inputs
    degree = jnp.arange(NDEG, dtype=jnp.int32)
    live_mask = degree[None, :] >= wave_block[:, None]
    even_mask = ((degree[None, :] + wave_block[:, None]) % 2) == 0
    coeffs = spec_block.astype(jnp.float32)
    nothing = jnp.zeros_like(coeffs)
    even_part = jnp.where((live_mask & even_mask)[None, None], coeffs, nothing)
    odd_part = jnp.where((live_mask & jnp.logical_not(even_mask))[None, None], coeffs, nothing)
    tables = table_block.astype(jnp.float32)
    highest = lax.Precision.HIGHEST
    sym_part = jnp.einsum("xcsn,skn->xcsk", even_part, tables, precision=highest)
    anti_part = jnp.einsum("xcsn,skn->xcsk", odd_part, tables, precision=highest)
    return jnp.concatenate([sym_part + anti_part, sym_part - anti_part], axis=3)


def reference(spectral, legendre, slot_wave, cycle_len, lat_order):
    blocks = 16
    width_block = MMAX // blocks
    spec_blocks = jnp.moveaxis(spectral.reshape(LEVELS, 2 * FIELDS, blocks, width_block, NDEG), 2, 0)
    table_blocks = legendre.reshape(blocks, width_block, LATH, NDEG)
    wave_blocks = slot_wave.reshape(blocks, width_block)
    fourier = lax.map(legendre_block, (spec_blocks, table_blocks, wave_blocks))
    fourier = jnp.moveaxis(fourier, 0, 2).reshape(LEVELS, 2 * FIELDS, MMAX, LATW)
    slots = jnp.arange(MMAX, dtype=jnp.int32)
    inverse = jnp.zeros((MMAX,), jnp.int32).at[slot_wave].set(slots)
    fourier_m = jnp.take(fourier, inverse, axis=2)

    def one_row(row):
        latitude = lat_order[row]
        length = cycle_len[latitude % LATH]
        coeffs = lax.dynamic_index_in_dim(fourier_m, latitude, axis=3, keepdims=False)
        coeffs = coeffs.reshape(LEVELS, FIELDS, 2, MMAX // 16, 16)
        placed = fold_cycle(coeffs, length)
        return jnp.transpose(placed.reshape(LEVELS * FIELDS, RPAD)).reshape(RPAD * LEVELS * FIELDS)

    return lax.map(one_row, jnp.arange(LATW, dtype=jnp.int32))
```

```python
import functools
import math

import jax
import jax.numpy as jnp
from jax import lax
from jax.experimental import pallas as pl
from jax.experimental.pallas import tpu as pltpu
from jax.sharding import PartitionSpec as P

RMAX = 5136
FIELDS = 3


def split(value):
    high = value.astype(jnp.bfloat16)
    return high, (value - high.astype(jnp.float32)).astype(jnp.bfloat16)


def dot_nt(left, right):
    return lax.dot_general(left, right, (((1,), (1,)), ((), ())), preferred_element_type=jnp.float32)


def turns(t):
    y = math.pi * t
    z = y * y
    sine = jnp.full_like(z, 1.0 / math.factorial(13))
    for n in (11, 9, 7, 5, 3, 1):
        sign = -1.0 if (n // 2) % 2 else 1.0
        sine = sine * z + sign / math.factorial(n)
    sine = sine * y
    cosine = jnp.full_like(z, 1.0 / math.factorial(12))
    for n in (10, 8, 6, 4, 2, 0):
        sign = -1.0 if (n // 2) % 2 else 1.0
        cosine = cosine * z + sign / math.factorial(n)
    return 1.0 - 2.0 * sine * sine, 2.0 * sine * cosine


def synth_kernel(step, step_pad, rows_dev, len_ref, inv_ref, wave_ref, coef_ref, out_ref, e_ref, w_ref, t_ref):
    lev_count = out_ref.shape[0]
    cycles, parts, slots = coef_ref.shape
    fields = parts // 2
    row_count = rows_dev * lev_count
    waves = wave_ref[...]
    weights = jnp.where(waves == 0.0, 1.0, 2.0)
    index = lax.broadcasted_iota(jnp.int32, (48, 1), 0)
    mult = jnp.where(
        index < 8,
        index,
        jnp.where(index < 24, 8 * (index - 8), jnp.where(index < 32, step * (index - 24), 8 * step * (index - 32))),
    ).astype(jnp.float32)
    products = waves * mult
    for r in range(cycles):
        length = len_ref[r]
        inverse = inv_ref[r]
        whole = jnp.floor(products * inverse + 0.5)
        cosine, sine = turns((products - whole * length) * inverse)
        for k in range(step_pad // 8):
            c0, s0, c1, s1 = cosine[0:8], sine[0:8], cosine[8 + k : 9 + k], sine[8 + k : 9 + k]
            e_ref[0, 8 * k : 8 * k + 8] = c0 * c1 - s0 * s1
            e_ref[1, 8 * k : 8 * k + 8] = s0 * c1 + c0 * s1
        for k in range((row_count + 15) // 16):
            tc, ts = [], []
            for h in (2 * k, 2 * k + 1):
                c0, s0, c1, s1 = cosine[24:32], sine[24:32], cosine[32 + h : 33 + h], sine[32 + h : 33 + h]
                tc.append(c0 * c1 - s0 * s1)
                ts.append(s0 * c1 + c0 * s1)
            for place, value in ((0, tc), (slots, ts)):
                high, low = split(jnp.concatenate(value, axis=0))
                t_ref[0, 16 * k : 16 * k + 16, place : place + slots] = high
                t_ref[1, 16 * k : 16 * k + 16, place : place + slots] = low
        for f in range(fields):
            real = coef_ref[r, 2 * f : 2 * f + 1] * weights
            imag = coef_ref[r, 2 * f + 1 : 2 * f + 2] * weights
            for k in range(step_pad // 16):
                ec = e_ref[0, 16 * k : 16 * k + 16]
                es = e_ref[1, 16 * k : 16 * k + 16]
                at = f * step_pad + 16 * k
                for place, value in ((0, real * ec - imag * es), (slots, -(real * es + imag * ec))):
                    high, low = split(value)
                    w_ref[0, at : at + 16, place : place + slots] = high
                    w_ref[1, at : at + 16, place : place + slots] = low
        total = dot_nt(t_ref[0], w_ref[0]) + dot_nt(t_ref[0], w_ref[1]) + dot_nt(t_ref[1], w_ref[0])
        shape = total.shape
        point = lax.broadcasted_iota(jnp.int32, shape, 0) * step + lax.broadcasted_iota(jnp.int32, shape, 1) % step_pad
        total = jnp.where(point.astype(jnp.float32) < length, total, 0.0)
        for d in range(lev_count):
            out_ref[d, r * rows_dev : (r + 1) * rows_dev] = total[d * rows_dev : (d + 1) * rows_dev]
    used = cycles * rows_dev
    if used < out_ref.shape[1]:
        out_ref[:, used:] = jnp.zeros((lev_count, out_ref.shape[1] - used, out_ref.shape[2]), jnp.float32)


def place_kernel(step, step_pad, rows_dev, cycles, x_ref, out_ref):
    lev_count, rows, width = x_ref.shape
    fields = width // step_pad
    group = lev_count * fields
    span = step * group
    span_pad = (span + 127) // 128 * 128
    source = lax.broadcasted_iota(jnp.int32, (width, 1), 0)
    shift = source % step_pad
    target = jnp.where(shift < step, shift * group + source // step_pad, -1)
    lane = lax.broadcasted_iota(jnp.int32, (width, span_pad), 1)
    chosen = jnp.where(lane == target, 1.0, 0.0).astype(jnp.bfloat16)
    values = x_ref[...].reshape(lev_count * rows, width)
    high, low = split(values)
    spread = jnp.dot(high, chosen, preferred_element_type=jnp.float32) + jnp.dot(
        low, chosen, preferred_element_type=jnp.float32
    )
    total = spread[:rows]
    for level in range(1, lev_count):
        total = total + pltpu.roll(spread[level * rows : (level + 1) * rows], fields * level, 1)
    for r in range(cycles):
        for q in range(rows_dev):
            row = r * rows_dev + q
            out_ref[r : r + 1, q * span : (q + 1) * span] = total[row : row + 1, :span]


def legendre_kernel(wave_ref, spec_ref, leg_ref, out_ref):
    parts, block, degrees = spec_ref.shape
    half_cycles = leg_ref.shape[0]
    table = leg_ref[...].reshape(half_cycles * block, degrees)
    waves = wave_ref[0]
    degree = lax.broadcasted_iota(jnp.int32, (block, degrees), 1)
    live = degree >= waves
    parity = (degree + waves) & 1
    even = (live & (parity == 0))[None]
    odd = (live & (parity == 1))[None]
    values = spec_ref[...].astype(jnp.float32)
    cells = parts * block
    shape = (half_cycles, block, cells)
    own = lax.broadcasted_iota(jnp.int32, shape, 1) == lax.broadcasted_iota(jnp.int32, shape, 2) % block
    sums = []
    for mask in (even, odd):
        part = jnp.where(mask, values, 0.0).reshape(cells, degrees).astype(jnp.bfloat16)
        product = dot_nt(table, part).reshape(shape)
        sums.append(jnp.sum(jnp.where(own, product, 0.0), axis=1))
    out_ref[0, 0] = sums[0] + sums[1]
    out_ref[0, 1] = sums[0] - sums[1]


def exchange_kernel(x_ref, out_ref, own_sem, send_sem, recv_sem):
    count = x_ref.shape[0]
    me = lax.axis_index("lev")
    barrier = pltpu.get_barrier_semaphore()
    for offset in range(1, count):
        peer = lax.rem(me + offset, count)
        pl.semaphore_signal(barrier, inc=1, device_id={"lev": peer}, device_id_type=pl.DeviceIdType.MESH)
    kept = pltpu.make_async_copy(x_ref.at[me], out_ref.at[me], own_sem)
    kept.start()
    pl.semaphore_wait(barrier, count - 1)
    copies = []
    for offset in range(1, count):
        peer = lax.rem(me + offset, count)
        copy = pltpu.make_async_remote_copy(
            src_ref=x_ref.at[peer],
            dst_ref=out_ref.at[me],
            send_sem=send_sem.at[offset],
            recv_sem=recv_sem.at[offset],
            device_id={"lev": peer},
            device_id_type=pl.DeviceIdType.MESH,
        )
        copy.start()
        copies.append(copy)
    kept.wait()
    for copy in copies:
        copy.wait()


def local(spectral, legendre, slot_wave, cycle_len, lat_order):
    slot_count = spectral.shape[2]
    degrees = spectral.shape[3]
    half_cycles = legendre.shape[1]
    wave_index = lax.axis_index("wave")
    lev_count = lax.axis_size("lev")
    wave_count = lax.axis_size("wave")
    slots = slot_wave.shape[0]
    padded_len = (RMAX + 8 * lev_count - 1) // (8 * lev_count) * 8 * lev_count
    points_dev = padded_len // lev_count
    step = max(b for b in range(8, 80, 8) if points_dev % b == 0)
    step_pad = (step + 15) // 16 * 16
    rows_dev = points_dev // step
    row_count = rows_dev * lev_count
    parts = spectral.shape[0] * spectral.shape[1]
    cycle_count = lat_order.shape[0] // wave_count

    local_waves = lax.dynamic_slice_in_dim(slot_wave, wave_index * slot_count, slot_count)
    block = 32 if slot_count % 32 == 0 else 16
    blocks = slot_count // block
    cells = parts * block
    fourier = pl.pallas_call(
        legendre_kernel,
        grid=(blocks,),
        out_shape=jax.ShapeDtypeStruct((blocks, 2, half_cycles, cells), jnp.float32),
        in_specs=[
            pl.BlockSpec((1, block, 1), lambda i: (i, 0, 0)),
            pl.BlockSpec((parts, block, degrees), lambda i: (0, i, 0)),
            pl.BlockSpec((half_cycles, block, degrees), lambda i: (0, i, 0)),
        ],
        out_specs=pl.BlockSpec((1, 2, half_cycles, cells), lambda i: (i, 0, 0, 0)),
        name="legendre",
    )(local_waves.reshape(blocks, block, 1), spectral.reshape(parts, slot_count, degrees), jnp.transpose(legendre, (1, 0, 2)))
    fourier = fourier.reshape(blocks, 2 * half_cycles, parts, block)
    fourier = jnp.transpose(fourier, (1, 2, 0, 3)).reshape(2 * half_cycles, parts * slot_count)
    ordered = jnp.take(fourier, lat_order, axis=0)
    ordered = ordered.reshape(wave_count, cycle_count, parts, slot_count)
    shared = lax.all_to_all(ordered, "wave", split_axis=0, concat_axis=0, tiled=True)
    coeffs = jnp.transpose(shared, (1, 2, 0, 3)).reshape(cycle_count, parts, slots)

    rows = wave_index * cycle_count + jnp.arange(cycle_count, dtype=jnp.int32)
    pairs = jnp.take(lat_order, rows) % half_cycles
    pair_match = pairs[:, None] == jnp.arange(half_cycles, dtype=jnp.int32)[None, :]
    lengths = jnp.sum(jnp.where(pair_match, cycle_len[None, :], 0), axis=1).astype(jnp.float32)
    waves = slot_wave.astype(jnp.float32)[None, :]
    send_rows = (cycle_count * rows_dev + 7) // 8 * 8
    width = parts // 2 * step_pad
    smem = pl.BlockSpec(memory_space=pltpu.SMEM)
    vmem = pl.BlockSpec(memory_space=pltpu.VMEM)
    row_pad = (row_count + 15) // 16 * 16
    points = pl.pallas_call(
        functools.partial(synth_kernel, step, step_pad, rows_dev),
        out_shape=jax.ShapeDtypeStruct((lev_count, send_rows, width), jnp.float32),
        in_specs=[smem, smem, vmem, vmem],
        out_specs=vmem,
        scratch_shapes=[
            pltpu.VMEM((2, step_pad, slots), jnp.float32),
            pltpu.VMEM((2, width, 2 * slots), jnp.bfloat16),
            pltpu.VMEM((2, row_pad, 2 * slots), jnp.bfloat16),
        ],
        name="synth",
    )(lengths, 1.0 / lengths, waves, coeffs)
    owned = pl.pallas_call(
        exchange_kernel,
        out_shape=jax.ShapeDtypeStruct(points.shape, jnp.float32),
        in_specs=[vmem],
        out_specs=vmem,
        scratch_shapes=[
            pltpu.SemaphoreType.DMA,
            pltpu.SemaphoreType.DMA((lev_count,)),
            pltpu.SemaphoreType.DMA((lev_count,)),
        ],
        compiler_params=pltpu.CompilerParams(collective_id=0, has_side_effects=True),
        name="exchange",
    )(points)
    return pl.pallas_call(
        functools.partial(place_kernel, step, step_pad, rows_dev, cycle_count),
        out_shape=jax.ShapeDtypeStruct((cycle_count, points_dev * lev_count * (parts // 2)), jnp.float32),
        in_specs=[vmem],
        out_specs=vmem,
        name="place",
    )(owned)


def solution(mesh):
    in_specs = (P("lev", None, "wave", None), P("wave", None, None), P(), P(), P())
    out_specs = P("wave", "lev")
    return jax.shard_map(local, mesh=mesh, in_specs=in_specs, out_specs=out_specs, check_vma=False)
```

```python
import functools
import math

import jax
import jax.numpy as jnp
from jax import lax
from jax.experimental import pallas as pl
from jax.experimental.pallas import tpu as pltpu
from jax.sharding import PartitionSpec as P

RMAX = 5136
FIELDS = 3


def split(value):
    high = value.astype(jnp.bfloat16)
    return high, (value - high.astype(jnp.float32)).astype(jnp.bfloat16)


def dot_nt(left, right):
    return lax.dot_general(left, right, (((1,), (1,)), ((), ())), preferred_element_type=jnp.float32)


def turns(t):
    y = math.pi * t
    z = y * y
    sine = jnp.full_like(z, 1.0 / math.factorial(13))
    for n in (11, 9, 7, 5, 3, 1):
        sign = -1.0 if (n // 2) % 2 else 1.0
        sine = sine * z + sign / math.factorial(n)
    sine = sine * y
    cosine = jnp.full_like(z, 1.0 / math.factorial(12))
    for n in (10, 8, 6, 4, 2, 0):
        sign = -1.0 if (n // 2) % 2 else 1.0
        cosine = cosine * z + sign / math.factorial(n)
    return 1.0 - 2.0 * sine * sine, 2.0 * sine * cosine


def points_kernel(
    step, step_pad, wave_ref, lat_ref, cycle_ref, coef_ref, out_ref,
    e_ref, w_ref, t_ref, place_ref, send_ref, got_ref, own_sem, send_sem, recv_sem,
):
    cycles, lev_count, rows_dev, wide = send_ref.shape
    parts, slots = coef_ref.shape[1:]
    fields = parts // 2
    half_cycles = cycle_ref.shape[0]
    me = lax.axis_index("lev")
    first_row = lax.axis_index("wave") * cycles
    barrier = pltpu.get_barrier_semaphore()
    for offset in range(1, lev_count):
        peer = lax.rem(me + offset, lev_count)
        pl.semaphore_signal(barrier, inc=1, device_id={"lev": peer}, device_id_type=pl.DeviceIdType.MESH)

    waves = wave_ref[...].astype(jnp.float32)
    weights = jnp.where(waves == 0.0, 1.0, 2.0)
    steps_e = (step_pad // 8 + 7) // 8 * 8
    steps_t = (lev_count + 7) // 8 * 8
    at_t = 8 + steps_e
    at_d = at_t + 8
    index = lax.broadcasted_iota(jnp.int32, (at_d + steps_t, 1), 0)
    mult = jnp.where(
        index < 8,
        index,
        jnp.where(index < at_t, 8 * (index - 8), jnp.where(index < at_d, step * (index - at_t), 8 * step * (index - at_d))),
    ).astype(jnp.float32)
    products = waves * mult
    copies = []
    for r in range(cycles):
        length = cycle_ref[lat_ref[first_row + r] % half_cycles].astype(jnp.float32)
        inverse = 1.0 / jnp.full((1, slots), length)
        whole = jnp.floor(products * inverse + 0.5)
        cosine, sine = turns((products - whole * length) * inverse)
        for k in range(step_pad // 8):
            c0, s0, c1, s1 = cosine[0:8], sine[0:8], cosine[8 + k : 9 + k], sine[8 + k : 9 + k]
            e_ref[0, 8 * k : 8 * k + 8] = c0 * c1 - s0 * s1
            e_ref[1, 8 * k : 8 * k + 8] = s0 * c1 + c0 * s1
        for k in range((lev_count + 1) // 2):
            tc, ts = [], []
            for d in (2 * k, 2 * k + 1):
                c0, s0 = cosine[at_t : at_d], sine[at_t : at_d]
                c1, s1 = cosine[at_d + d : at_d + d + 1], sine[at_d + d : at_d + d + 1]
                tc.append(c0 * c1 - s0 * s1)
                ts.append(s0 * c1 + c0 * s1)
            for place, value in ((0, tc), (slots, ts)):
                high, low = split(jnp.concatenate(value, axis=0))
                t_ref[0, 16 * k : 16 * k + 16, place : place + slots] = high
                t_ref[1, 16 * k : 16 * k + 16, place : place + slots] = low
        for f in range(fields):
            real = coef_ref[r, 2 * f : 2 * f + 1] * weights
            imag = coef_ref[r, 2 * f + 1 : 2 * f + 2] * weights
            for k in range(step_pad // 16):
                ec = e_ref[0, 16 * k : 16 * k + 16]
                es = e_ref[1, 16 * k : 16 * k + 16]
                at = f * step_pad + 16 * k
                for place, value in ((0, real * ec - imag * es), (slots, -(real * es + imag * ec))):
                    high, low = split(value)
                    w_ref[0, at : at + 16, place : place + slots] = high
                    w_ref[1, at : at + 16, place : place + slots] = low
        total = dot_nt(t_ref[0], w_ref[0]) + dot_nt(t_ref[0], w_ref[1]) + dot_nt(t_ref[1], w_ref[0])
        shape = total.shape
        point = lax.broadcasted_iota(jnp.int32, shape, 0) * step + lax.broadcasted_iota(jnp.int32, shape, 1) % step_pad
        total = jnp.where(point.astype(jnp.float32) < length, total, 0.0)[: lev_count * rows_dev]
        pieces = [total[:, f * step_pad : f * step_pad + step] for f in range(fields)]
        if wide > fields * step:
            pieces.append(jnp.zeros((lev_count * rows_dev, wide - fields * step), jnp.float32))
        send_ref[r] = jnp.concatenate(pieces, axis=1).reshape(lev_count, rows_dev, wide)
        if r == 0:
            pl.semaphore_wait(barrier, lev_count - 1)
        started = []
        for offset in range(1, lev_count):
            peer = lax.rem(me + offset, lev_count)
            copy = pltpu.make_async_remote_copy(
                src_ref=send_ref.at[r, peer],
                dst_ref=got_ref.at[r, me],
                send_sem=send_sem.at[r, offset],
                recv_sem=recv_sem.at[r, offset],
                device_id={"lev": peer},
                device_id_type=pl.DeviceIdType.MESH,
            )
            copy.start()
            started.append(copy)
        kept = pltpu.make_async_copy(send_ref.at[r, me], got_ref.at[r, me], own_sem.at[r])
        kept.start()
        started.append(kept)
        copies.append(started)

    group = lev_count * fields
    span = step * group
    source = lax.broadcasted_iota(jnp.int32, (wide, 1), 0)
    target = jnp.where(source < fields * step, (source % step) * group + source // step, -1)
    lane = lax.broadcasted_iota(jnp.int32, place_ref.shape, 1)
    place_ref[...] = jnp.where(lane == target, 1.0, 0.0).astype(jnp.bfloat16)
    for r in range(cycles):
        for copy in copies[r]:
            copy.wait()
        high, low = split(got_ref[r].reshape(lev_count * rows_dev, wide))
        spread = jnp.dot(high, place_ref[...], preferred_element_type=jnp.float32) + jnp.dot(
            low, place_ref[...], preferred_element_type=jnp.float32
        )
        total = spread[:rows_dev]
        for level in range(1, lev_count):
            total = total + pltpu.roll(spread[level * rows_dev : (level + 1) * rows_dev], fields * level, 1)
        for q in range(rows_dev):
            out_ref[r : r + 1, q * span : (q + 1) * span] = total[q : q + 1, :span]


def legendre_kernel(wave_ref, spec_ref, leg_ref, out_ref):
    parts, block, degrees = spec_ref.shape
    half_cycles = leg_ref.shape[0]
    table = leg_ref[...].reshape(half_cycles * block, degrees)
    waves = wave_ref[0]
    degree = lax.broadcasted_iota(jnp.int32, (block, degrees), 1)
    live = degree >= waves
    parity = (degree + waves) & 1
    values = spec_ref[...]
    cells = parts * block
    shape = (half_cycles, block, cells)
    own = lax.broadcasted_iota(jnp.int32, shape, 1) == lax.broadcasted_iota(jnp.int32, shape, 2) % block
    sums = []
    for which in (0, 1):
        mask = jnp.where(live & (parity == which), 1.0, 0.0).astype(jnp.bfloat16)
        part = (values * mask[None]).reshape(cells, degrees)
        product = dot_nt(table, part).reshape(shape)
        sums.append(jnp.sum(jnp.where(own, product, 0.0), axis=1))
    out_ref[0, 0] = sums[0] + sums[1]
    out_ref[0, 1] = sums[0] - sums[1]


def local(spectral, legendre, slot_wave, cycle_len, lat_order):
    slot_count = spectral.shape[2]
    degrees = spectral.shape[3]
    half_cycles = legendre.shape[1]
    wave_index = lax.axis_index("wave")
    lev_count = lax.axis_size("lev")
    wave_count = lax.axis_size("wave")
    slots = slot_wave.shape[0]
    padded_len = (RMAX + 8 * lev_count - 1) // (8 * lev_count) * 8 * lev_count
    points_dev = padded_len // lev_count
    step = points_dev // 8
    step_pad = (step + 15) // 16 * 16
    parts = spectral.shape[0] * spectral.shape[1]
    cycle_count = lat_order.shape[0] // wave_count

    local_waves = lax.dynamic_slice_in_dim(slot_wave, wave_index * slot_count, slot_count)
    block = 32 if slot_count % 32 == 0 else 16
    blocks = slot_count // block
    cells = parts * block
    fourier = pl.pallas_call(
        legendre_kernel,
        grid=(blocks,),
        out_shape=jax.ShapeDtypeStruct((blocks, 2, half_cycles, cells), jnp.float32),
        in_specs=[
            pl.BlockSpec((1, block, 1), lambda i: (i, 0, 0)),
            pl.BlockSpec((parts, block, degrees), lambda i: (0, i, 0)),
            pl.BlockSpec((half_cycles, block, degrees), lambda i: (0, i, 0)),
        ],
        out_specs=pl.BlockSpec((1, 2, half_cycles, cells), lambda i: (i, 0, 0, 0)),
        name="legendre",
    )(local_waves.reshape(blocks, block, 1), spectral.reshape(parts, slot_count, degrees), jnp.transpose(legendre, (1, 0, 2)))
    fourier = fourier.reshape(blocks, 2 * half_cycles, parts, block)
    fourier = jnp.transpose(fourier, (1, 2, 0, 3)).reshape(2 * half_cycles, parts * slot_count)
    ordered = jnp.take(fourier, lat_order, axis=0, mode="clip")
    ordered = ordered.reshape(wave_count, cycle_count, parts, slot_count)
    shared = lax.all_to_all(ordered, "wave", split_axis=0, concat_axis=0, tiled=True)
    coeffs = jnp.transpose(shared, (1, 2, 0, 3)).reshape(cycle_count, parts, slots)

    wide = (parts // 2 * step + 127) // 128 * 128
    span = (parts // 2 * lev_count * step + 127) // 128 * 128
    smem = pl.BlockSpec(memory_space=pltpu.SMEM)
    vmem = pl.BlockSpec(memory_space=pltpu.VMEM)
    row_pad = (lev_count + 1) // 2 * 16
    return pl.pallas_call(
        functools.partial(points_kernel, step, step_pad),
        out_shape=jax.ShapeDtypeStruct((cycle_count, points_dev * lev_count * (parts // 2)), jnp.float32),
        in_specs=[vmem, smem, smem, vmem],
        out_specs=vmem,
        scratch_shapes=[
            pltpu.VMEM((2, step_pad, slots), jnp.float32),
            pltpu.VMEM((2, parts // 2 * step_pad, 2 * slots), jnp.bfloat16),
            pltpu.VMEM((2, row_pad, 2 * slots), jnp.bfloat16),
            pltpu.VMEM((wide, span), jnp.bfloat16),
            pltpu.VMEM((cycle_count, lev_count, 8, wide), jnp.float32),
            pltpu.VMEM((cycle_count, lev_count, 8, wide), jnp.float32),
            pltpu.SemaphoreType.DMA((cycle_count,)),
            pltpu.SemaphoreType.DMA((cycle_count, lev_count)),
            pltpu.SemaphoreType.DMA((cycle_count, lev_count)),
        ],
        compiler_params=pltpu.CompilerParams(collective_id=0, has_side_effects=True),
        name="points",
    )(slot_wave[None, :], lat_order, cycle_len, coeffs)


def solution(mesh):
    in_specs = (P("lev", None, "wave", None), P("wave", None, None), P(), P(), P())
    out_specs = P("wave", "lev")
    return jax.shard_map(local, mesh=mesh, in_specs=in_specs, out_specs=out_specs, check_vma=False)
```
